256 devices in a mesh: seq: 64 (over z, x, core), mp: 4 (over y).
Axes of the slice: x: 4, y: 4, z: 8, core: 2. Of those that a mesh axis runs over, the one named last changes fastest.
Arguments:
- x_in: bfloat16 [8192, 8192], P('seq', 'mp'), may hold values from -6 to 6
- gate_z: bfloat16 [8192, 8192], P('seq', 'mp'), may hold values from -6 to 6
- bc_in: bfloat16 [8192, 256], P('seq'), may hold values from -3 to 3
- dt_raw: float32 [8192, 128], P('seq', 'mp'), may hold values from -9 to 0
- a_log: float32 [128], P('mp'), may hold values from -9 to -1
- d_skip: float32 [128], P('mp'), may hold values from 0.5 to 1.5
- conv_x: bfloat16 [4, 8192], P(None, 'mp'), may hold values from -3 to 3
- conv_bc: bfloat16 [4, 256], replicated, may hold values from -3 to 3
- norm_gain: float32 [8192], P('mp'), may hold values from 0.1 to 1.9
- queries: bfloat16 [8192, 4096], P('seq', 'mp'), may hold values from -12 to 12
- key_value_pairs: bfloat16 [2, 8192, 512], P(None, 'seq', 'mp'), may hold values from -12 to 12
Outputs:
- mixer_out: bfloat16 [8192, 8192], P('seq', 'mp')
- attention_out: bfloat16 [8192, 4096], P('seq', 'mp')
The draws below stay inside these ranges and needn't reach their ends.
All inputs are finite; a program needn't handle non-finite values.
Results may differ from the reference program's by a relative error of at most 0.00085.
Values may be sent and summed in bfloat16 or wider, within the bound.
A program may use at most 192 MiB of HBM per device.

```python
import math
import jax
import jax.numpy as jnp
from jax import lax

TOK_DEV = 128
HEADS = 128
HEAD_P = 64
STATE = 128
CONV = 4
QUERY_HEADS = 32
KEY_VALUE_HEADS = 4
HEAD_WIDTH = 128
D_INNER = 8192
TOKEN_COUNT = 8192


def decay_plan(key):
    base_key = jax.random.fold_in(key, 7)
    k_class, k_slow, k_fast, k_block, k_token = jax.random.split(base_key, 5)
    share = 0.5
    slow = jax.random.uniform(k_class, (HEADS,)) < share
    root = jnp.sqrt(jnp.float32(TOKEN_COUNT))
    rate_slow = jnp.exp(jax.random.uniform(k_slow, (HEADS,), jnp.float32, math.log(0.3), 0.0)) / root
    rate_fast = jnp.exp(jax.random.uniform(k_fast, (HEADS,), jnp.float32, math.log(0.08), math.log(0.16)))
    rate = jnp.where(slow, rate_slow, rate_fast)
    level = jnp.where(slow, 1.0 / root, 0.25)
    return (rate, level, k_block, k_token)


def draw_a_log(key, part):
    rate, level, k_block, k_token = decay_plan(key)
    return jnp.log(rate).astype(jnp.float32)


def draw_dt_raw(key, part):
    rate, level, k_block, k_token = decay_plan(key)
    blocks = TOKEN_COUNT // TOK_DEV
    block_factor = jnp.exp(jax.random.uniform(k_block, (blocks, 1, HEADS), jnp.float32, math.log(0.6), math.log(1.2)))
    block_factor = jnp.broadcast_to(block_factor, (blocks, TOK_DEV, HEADS)).reshape(TOKEN_COUNT, HEADS)
    token_factor = jnp.exp(jax.random.uniform(k_token, (TOKEN_COUNT, HEADS), jnp.float32, math.log(0.5), math.log(1.5)))
    step = level[None, :] * block_factor * token_factor
    return (step + jnp.log(-jnp.expm1(-step))).astype(jnp.float32)


def attention_plan(key):
    base_key = jax.random.fold_in(key, 11)
    k_query, key_block_rows = jax.random.split(base_key, 2)
    query_part = jnp.clip(jax.random.normal(k_query, (TOKEN_COUNT, QUERY_HEADS * HEAD_WIDTH), jnp.float32), -6.0, 6.0)
    key_segment = jnp.clip(jax.random.normal(key_block_rows, (2, TOKEN_COUNT, KEY_VALUE_HEADS * HEAD_WIDTH), jnp.float32), -6.0, 6.0)
    return (query_part, key_segment)


def draw_queries(key, part):
    query_part, key_segment = attention_plan(key)
    return query_part.astype(jnp.bfloat16)


def draw_key_value_pairs(key, part):
    query_part, key_segment = attention_plan(key)
    return key_segment.astype(jnp.bfloat16)


def block_levels(key, extent, cuts, least, largest):
    factor_of, own = 1.0, jax.random.fold_in(key, 6)
    for axis_at, parts in cuts:
        heights = jnp.exp(jax.random.uniform(jax.random.fold_in(own, axis_at), (parts,), jnp.float32, least / len(cuts), largest / len(cuts)))
        factor_of = factor_of * jnp.repeat(heights, extent[axis_at] // parts).reshape([-1 if axis == axis_at else 1 for axis in range(len(extent))])
    return factor_of


def gaussian(stream_key, shape, scale, bound, cuts=(), kind=jnp.bfloat16):
    drawn = jax.random.normal(stream_key, shape, jnp.float32) * scale
    if len(cuts) > 0:
        drawn = block_levels(stream_key, shape, cuts, -0.22, 0.18) * drawn
    return jnp.clip(drawn, min=-bound, max=bound).astype(kind)


def setup_inputs(seed: int = 0) -> dict:
    streams_of = jax.random.split(jax.random.key(seed), 12)
    return {
        "x_in": gaussian(streams_of[0], (TOKEN_COUNT, D_INNER), 1.0, 6.0, ((0, 64), (1, 4))),
        "gate_z": gaussian(streams_of[1], (TOKEN_COUNT, D_INNER), 1.0, 6.0, ((0, 64), (1, 4))),
        "bc_in": gaussian(streams_of[2], (TOKEN_COUNT, 2 * STATE), 0.5, 3.0, ((0, 64),)),
        "dt_raw": draw_dt_raw(jax.random.fold_in(streams_of[11], 71), 0),
        "a_log": draw_a_log(jax.random.fold_in(streams_of[11], 71), 0),
        "d_skip": jnp.clip(0.5 + 1.0 * jax.random.uniform(streams_of[5], (HEADS,), jnp.float32) ** block_levels(streams_of[5], (HEADS,), ((0, 4),), -0.2, 0.2), 0.5, 1.5),
        "conv_x": gaussian(streams_of[6], (CONV, D_INNER), CONV ** -0.5, 3.0, ((1, 4),)),
        "conv_bc": gaussian(streams_of[7], (CONV, 2 * STATE), CONV ** -0.5, 3.0),
        "norm_gain": jnp.clip(1.0 + 0.18 * jax.random.normal(streams_of[8], (D_INNER,), jnp.float32), 0.1, 1.9),
        "queries": draw_queries(jax.random.fold_in(streams_of[11], 71), 0),
        "key_value_pairs": draw_key_value_pairs(jax.random.fold_in(streams_of[11], 71), 0),
    }


def causal_conv(values, taps):
    padded = jnp.pad(values.astype(jnp.float32), ((CONV - 1, 0), (0, 0)))
    total = jnp.zeros((values.shape[0], values.shape[1]), jnp.float32)
    for k in range(CONV):
        total = total + taps[k].astype(jnp.float32)[None, :] * padded[k:k + values.shape[0]]
    return jax.nn.silu(total)

def local_part(xs, b_map, c_map, step, rate):
    hi = lax.Precision.HIGHEST
    cum = jnp.cumsum(step * rate[None, :], axis=0)
    rows = xs.shape[0]
    order = jnp.arange(rows)
    causal = order[None, :] <= order[:, None]
    inner = jnp.dot(c_map, b_map.T, precision=hi)
    cum_t = cum.T
    diff = cum_t[:, :, None] - cum_t[:, None, :]
    decay = jnp.where(causal[None], jnp.exp(jnp.where(causal[None], diff, 0.0)), 0.0)
    mixing = inner[None] * decay
    scaled = step[:, :, None] * xs
    y_intra = jnp.einsum('hts,shp->thp', mixing, scaled, precision=hi)
    to_end = jnp.exp(cum[-1][None, :] - cum)
    s_loc = jnp.einsum('sn,shp->hnp', b_map, scaled * to_end[:, :, None], precision=hi)
    return (y_intra, s_loc, jnp.exp(cum[-1]), cum)

def inter_part(c_map, cum, state_in):
    hi = lax.Precision.HIGHEST
    return jnp.exp(cum)[:, :, None] * jnp.einsum('tn,hnp->thp', c_map, state_in, precision=hi)

def reference(x_in, gate_z, bc_in, dt_raw, a_log, d_skip, conv_x, conv_bc, norm_gain, queries, key_value_pairs):
    xs = causal_conv(x_in, conv_x).reshape(TOKEN_COUNT, HEADS, HEAD_P)
    bc_conv = causal_conv(bc_in, conv_bc)
    step = jax.nn.softplus(dt_raw)
    rate = -jnp.exp(a_log)
    blocks = TOKEN_COUNT // TOK_DEV
    data = (xs.reshape(blocks, TOK_DEV, HEADS, HEAD_P), bc_conv[:, :STATE].reshape(blocks, TOK_DEV, STATE), bc_conv[:, STATE:].reshape(blocks, TOK_DEV, STATE), step.reshape(blocks, TOK_DEV, HEADS))

    def advance(state, item):
        xb, bb, cb, sb = item
        y_intra, s_loc, g_end, cum = local_part(xb, bb, cb, sb, rate)
        y_block = y_intra + inter_part(cb, cum, state)
        return (g_end[:, None, None] * state + s_loc, y_block)
    _, outs = lax.scan(advance, jnp.zeros((HEADS, STATE, HEAD_P), jnp.float32), data)
    y_all = outs.reshape(TOKEN_COUNT, HEADS, HEAD_P) + d_skip[None, :, None] * xs
    gated = y_all.reshape(TOKEN_COUNT, D_INNER) * jax.nn.silu(gate_z.astype(jnp.float32))
    mean_sq = lax.optimization_barrier(jnp.mean(gated * gated, axis=1, keepdims=True))
    mixer_out = (gated * lax.rsqrt(mean_sq + 1e-05) * norm_gain[None, :]).astype(jnp.bfloat16)
    query_group = QUERY_HEADS // KEY_VALUE_HEADS
    scale = HEAD_WIDTH ** (-0.5)
    every_query = queries.astype(jnp.float32).reshape(TOKEN_COUNT, KEY_VALUE_HEADS, query_group, HEAD_WIDTH)
    every_key = key_value_pairs[0].astype(jnp.float32).reshape(TOKEN_COUNT, KEY_VALUE_HEADS, HEAD_WIDTH)
    every_value = key_value_pairs[1].astype(jnp.float32).reshape(TOKEN_COUNT, KEY_VALUE_HEADS, HEAD_WIDTH)
    qblock = min(512, TOKEN_COUNT)
    pieces = []
    for b in range(TOKEN_COUNT // qblock):
        kend = (b + 1) * qblock
        q_blk = every_query[b * qblock:kend]
        score = jnp.einsum('qhgd,khd->hgqk', q_blk, every_key[:kend]) * scale
        live = jnp.arange(kend)[None, :] <= (b * qblock + jnp.arange(qblock))[:, None]
        score = jnp.where(live[None, None], score, -1e+30)
        peak = lax.optimization_barrier(jnp.max(score, axis=-1, keepdims=True))
        weights = jnp.where(live[None, None], jnp.exp(score - peak), 0.0)
        total = lax.optimization_barrier(jnp.sum(weights, axis=-1))
        mixed = jnp.einsum('hgqk,khd->qhgd', weights, every_value[:kend])
        mixed = mixed / jnp.transpose(total, (2, 0, 1))[:, :, :, None]
        pieces.append(mixed.reshape(qblock, QUERY_HEADS * HEAD_WIDTH))
    attention_out = jnp.concatenate(pieces, axis=0).astype(jnp.bfloat16)
    return (mixer_out, attention_out)
```

```python
import jax
import jax.numpy as jnp
from jax import lax
from jax.experimental import pallas as pl
from jax.experimental.pallas import tpu as pltpu
from jax.sharding import PartitionSpec as P

HEAD_P = 64
STATE = 128
CONV = 4
HEAD_WIDTH = 128
D_INNER = 8192

ROWS = 128
PLANE = 8
PLANES = 8
CHIPS = 4
TOK = PLANE * ROWS
WIDE = 256
OWN_HEADS = 4
TAIL = 16
Q_HEADS = 8
SPLIT = 16

MESH = pl.DeviceIdType.MESH
F32 = jnp.float32
BF16 = jnp.bfloat16
HI = lax.Precision.HIGHEST
NN = (((1,), (0,)), ((), ()))
NT = (((1,), (1,)), ((), ()))


def dot1(a, b, dims=NN):
    return lax.dot_general(a, b, dims, preferred_element_type=F32)


def exact(a, b, dims=NN):
    return lax.dot_general(a, b, dims, precision=HI, preferred_element_type=F32)


def halves(v):
    high = v.astype(BF16)
    return high, (v - high.astype(F32)).astype(BF16)


def dot3(a, b, dims=NN):
    ah, al = halves(a)
    bh, bl = halves(b)
    return dot1(ah, bh, dims) + (dot1(ah, bl, dims) + dot1(al, bh, dims))


def silu(v):
    return v / (1.0 + jnp.exp(-v))


def softplus(v):
    u = jnp.exp(-jnp.abs(v))
    w = 1.0 + u
    small = w == 1.0
    tail = jnp.where(small, u, jnp.log(w) * (u / jnp.where(small, 1.0, w - 1.0)))
    return jnp.maximum(v, 0.0) + tail


def kernel(
    x_hbm,
    gate_hbm,
    bc_hbm,
    dt_ref,
    alog_ref,
    dskip_ref,
    taps_x_ref,
    taps_bc_ref,
    gain_ref,
    q_hbm,
    kv_hbm,
    mix_hbm,
    att_hbm,
    kvbuf,
    xbuf,
    gbuf,
    bcbuf,
    dtsrc,
    dtbuf,
    xs_ref,
    b_ref,
    c_ref,
    cum_ref,
    step_ref,
    lead_ref,
    states,
    y_ref,
    tsrc,
    trecv,
    psrc,
    precv,
    ss_ref,
    ssm_ref,
    ss2_ref,
    ssp_ref,
    osrc,
    qbuf,
    peak_ref,
    acc_ref,
    obuf,
    local_sem,
    q_sem,
    x_s,
    x_r,
    dt_s,
    dt_r,
    g_s,
    g_r,
    bcx_s,
    bcx_r,
    bcp_s,
    bcp_r,
    kvx_s,
    kvx_r,
    kvp_s,
    kvp_r,
    up_s,
    up_r,
    dn_s,
    dn_r,
    tx_s,
    tb_s,
    tail_r,
    t_s,
    t_r,
    p_s,
    p_r,
    m_s,
    m_r,
    n_s,
    n_r,
    o_s,
    o_r,
):
    me = lax.axis_index("seq")
    mine_mp = lax.axis_index("mp")
    z = me // PLANE
    j = me % PLANE
    xc = j // 2
    core = j % 2
    base = z * PLANE
    partner = base + xc * 2 + (1 - core)
    above = ((z + 1) % PLANES) * PLANE
    below = ((z + PLANES - 1) % PLANES) * PLANE

    def remote(src, dst, ss, rs, seq):
        return pltpu.make_async_remote_copy(
            src_ref=src, dst_ref=dst, send_sem=ss, recv_sem=rs, device_id={"seq": seq}, device_id_type=MESH
        )

    def in_plane(r):
        return base + (j + r) % PLANE

    def on_chip(r):
        return base + ((xc + r) % CHIPS) * 2 + core

    def in_column(r):
        return ((z + r) % PLANES) * PLANE + j

    def from_plane(r):
        return (j + PLANE - r) % PLANE

    def from_column(r):
        return (z + PLANES - r) % PLANES

    barrier = pltpu.get_barrier_semaphore()

    def greet(seq):
        pl.semaphore_signal(barrier, inc=1, device_id={"seq": seq}, device_id_type=MESH)

    @pl.loop(1, PLANE)
    def _(r):
        greet(in_plane(r))
        greet(in_column(r))

    @pl.loop(1, 4)
    def _(r):
        pl.semaphore_signal(barrier, inc=1, device_id={"mp": (mine_mp + r) % 4}, device_id_type=MESH)

    @pl.when(j == PLANE - 1)
    def _():
        @pl.loop(0, PLANE - 1)
        def _(d):
            greet(above + d)

    @pl.when(j != PLANE - 1)
    def _():
        greet(below + PLANE - 1)

    dt_t = jnp.transpose(dt_ref[...])
    for d in range(PLANE):
        dtsrc[d, pl.ds(0, OWN_HEADS), :] = dt_t[d * OWN_HEADS : (d + 1) * OWN_HEADS]
        dtsrc[d, pl.ds(OWN_HEADS, OWN_HEADS), :] = jnp.zeros((OWN_HEADS, ROWS), F32)

    my_rows = pl.ds(pl.multiple_of(TAIL + j * ROWS, TAIL), ROWS)
    kv_off = pl.multiple_of(core * 512 + xc * ROWS, ROWS)
    kv_mine = kvbuf.at[z, :, pl.ds(kv_off, ROWS), :]

    def cols(d):
        return pl.ds(pl.multiple_of(d * WIDE, WIDE), WIDE)

    local = [
        pltpu.make_async_copy(kv_hbm, kv_mine, local_sem.at[0]),
        pltpu.make_async_copy(bc_hbm, bcbuf.at[my_rows, :], local_sem.at[1]),
        pltpu.make_async_copy(x_hbm.at[:, cols(j)], xbuf.at[my_rows, :], local_sem.at[2]),
        pltpu.make_async_copy(dtsrc.at[j], dtbuf.at[j], local_sem.at[3]),
        pltpu.make_async_copy(
            gate_hbm.at[:, cols(j)], gbuf.at[pl.ds(pl.multiple_of(j * ROWS, ROWS), ROWS), :], local_sem.at[4]
        ),
    ]
    for copy in local:
        copy.start()
    for h in range(Q_HEADS):
        pltpu.make_async_copy(q_hbm.at[:, pl.ds(h * 128, 128)], qbuf.at[pl.ds(h * ROWS, ROWS), :], q_sem.at[h]).start()

    pl.semaphore_wait(barrier, 2 * (PLANE - 1) + 3 + jnp.where(j == PLANE - 1, PLANE - 1, 1))

    def kvx(r):
        return remote(kv_hbm, kv_mine, kvx_s.at[r], kvx_r.at[r], on_chip(r))

    def kvx_in(r):
        off = pl.multiple_of(core * 512 + ((xc + CHIPS - r) % CHIPS) * ROWS, ROWS)
        slot = kvbuf.at[z, :, pl.ds(off, ROWS), :]
        return remote(slot, slot, kvx_s.at[r], kvx_r.at[r], partner)

    def bcx(r):
        return remote(bc_hbm, bcbuf.at[my_rows, :], bcx_s.at[r], bcx_r.at[r], on_chip(r))

    def bc_slot(r, half):
        owner = ((xc + CHIPS - r) % CHIPS) * 2 + half
        return bcbuf.at[pl.ds(pl.multiple_of(TAIL + owner * ROWS, TAIL), ROWS), :]

    def bcx_in(r):
        slot = bc_slot(r, core)
        return remote(slot, slot, bcx_s.at[r], bcx_r.at[r], partner)

    def bcp(r):
        slot = bc_slot(r, core)
        return remote(slot, slot, bcp_s.at[r], bcp_r.at[r], partner)

    def bcp_in(r):
        slot = bc_slot(r, 1 - core)
        return remote(slot, slot, bcp_s.at[r], bcp_r.at[r], partner)

    bcp_own = remote(bc_hbm, bcbuf.at[my_rows, :], bcp_s.at[0], bcp_r.at[0], partner)

    def xa(r):
        return remote(
            x_hbm.at[:, cols((j + r) % PLANE)], xbuf.at[my_rows, :], x_s.at[r], x_r.at[r], in_plane(r)
        )

    def xa_in(r):
        slot = xbuf.at[pl.ds(pl.multiple_of(TAIL + from_plane(r) * ROWS, TAIL), ROWS), :]
        return remote(slot, slot, x_s.at[r], x_r.at[r], in_plane(r))

    def dta(r):
        return remote(dtsrc.at[(j + r) % PLANE], dtbuf.at[j], dt_s.at[r], dt_r.at[r], in_plane(r))

    def dta_in(r):
        slot = dtbuf.at[from_plane(r)]
        return remote(slot, slot, dt_s.at[r], dt_r.at[r], in_plane(r))

    def ga(r):
        slot = gbuf.at[pl.ds(pl.multiple_of(j * ROWS, ROWS), ROWS), :]
        return remote(gate_hbm.at[:, cols((j + r) % PLANE)], slot, g_s.at[r], g_r.at[r], in_plane(r))

    def ga_in(r):
        slot = gbuf.at[pl.ds(pl.multiple_of(from_plane(r) * ROWS, ROWS), ROWS), :]
        return remote(slot, slot, g_s.at[r], g_r.at[r], in_plane(r))

    last_rows = pl.ds(ROWS - TAIL, TAIL)

    def tail_x(d):
        return remote(
            x_hbm.at[last_rows, cols(d)], xbuf.at[pl.ds(0, TAIL), :], tx_s.at[d], tail_r.at[0], above + d
        )

    def tail_bc(d):
        return remote(
            bc_hbm.at[last_rows, :], bcbuf.at[pl.ds(0, TAIL), :], tb_s.at[d], tail_r.at[1], above + d
        )

    @pl.loop(1, CHIPS)
    def _(r):
        kvx(r).start()

    @pl.loop(1, CHIPS)
    def _(r):
        bcx(r).start()

    bcp_own.start()

    @pl.when(j == PLANE - 1)
    def _():
        @pl.loop(0, PLANE)
        def _(d):
            tail_x(d).start()
            tail_bc(d).start()

    @pl.loop(1, PLANE)
    def _(r):
        dta(r).start()
        xa(r).start()

    @pl.loop(1, PLANE)
    def _(r):
        ga(r).start()

    def column(zz, half):
        return kvbuf.at[zz, :, pl.ds(pl.multiple_of(half * 512, 512), 512), :]

    def up(s):
        part = column((z + PLANES - s + 1) % PLANES, core)
        return remote(part, part, up_s.at[s], up_r.at[s], above + j)

    def up_in(s):
        part = column((z + PLANES - s) % PLANES, core)
        return remote(part, part, up_s.at[s], up_r.at[s], above + j)

    def down(s):
        part = column((z + s - 1) % PLANES, core)
        return remote(part, part, dn_s.at[s], dn_r.at[s], below + j)

    def down_in(s):
        part = column((z + s) % PLANES, core)
        return remote(part, part, dn_s.at[s], dn_r.at[s], below + j)

    def share(zz, i):
        part = column(zz, core)
        return remote(part, part, kvp_s.at[i], kvp_r.at[i], partner)

    def share_in(zz, i):
        part = column(zz, 1 - core)
        return remote(part, part, kvp_s.at[i], kvp_r.at[i], partner)

    local[0].wait()

    @pl.loop(1, CHIPS)
    def _(r):
        kvx_in(r).wait_recv()

    up(1).start()
    down(1).start()
    share(z, 0).start()

    def ring_step(s):
        up_in(s).wait_recv()
        if s < 4:
            up(s + 1).start()
        share((z + PLANES - s) % PLANES, s).start()
        if s < 4:
            down_in(s).wait_recv()
            if s < 3:
                down(s + 1).start()
            share((z + s) % PLANES, 8 - s).start()

    factor = (HEAD_WIDTH ** (-0.5)) * 1.4426950408889634
    tile = 256

    def attend(zz, own):
        @pl.loop(0, Q_HEADS * ROWS // tile)
        def _(t):
            rows = pl.ds(pl.multiple_of(t * tile, tile), tile)
            q = qbuf[rows, :]
            score = dot1(q, kvbuf[zz, 0], NT)
            if own:
                lane = lax.broadcasted_iota(jnp.int32, (1, TOK), 1)
                spot = (((lane % 512) // ROWS) * 2 + lane // 512) * ROWS + lane % ROWS
                place = j * ROWS + lax.broadcasted_iota(jnp.int32, (tile, 1), 0) % ROWS
                score = jnp.where(spot <= place, score, -1e30)
                peak = jnp.max(score, axis=1, keepdims=True)
            else:
                before = peak_ref[rows, :][:, :1]
                peak = jnp.maximum(before, jnp.max(score, axis=1, keepdims=True))
            weights = jnp.exp2((score - peak) * factor)
            high, low = halves(weights)
            value = jnp.concatenate([kvbuf[zz, 1], jnp.ones((TOK, HEAD_WIDTH), BF16)], axis=1)
            part = dot1(high, value) + dot1(low, value)
            if own:
                acc_ref[rows, :] = part
            else:
                acc_ref[rows, :] = acc_ref[rows, :] * jnp.exp2((before - peak) * factor) + part
            peak_ref[rows, :] = jnp.broadcast_to(peak, (tile, HEAD_WIDTH))

    def attend_step(i):
        zz = (z + PLANES - i) % PLANES
        share_in(zz, i).wait_recv()

        @pl.when(i <= z)
        def _():
            attend(zz, False)

    for h in range(Q_HEADS):
        pltpu.make_async_copy(q_hbm.at[:, pl.ds(h * 128, 128)], qbuf.at[pl.ds(h * ROWS, ROWS), :], q_sem.at[h]).wait()
    share_in(z, 0).wait_recv()

    local[1].wait()

    @pl.loop(1, CHIPS)
    def _(r):
        bcx_in(r).wait_recv()
        bcp(r).start()

    attend(z, True)

    @pl.loop(0, CHIPS)
    def _(r):
        bcp_in(r).wait_recv()

    tail_x_in = remote(
        xbuf.at[pl.ds(0, TAIL), :], xbuf.at[pl.ds(0, TAIL), :], tx_s.at[0], tail_r.at[0], partner
    )
    tail_bc_in = remote(
        bcbuf.at[pl.ds(0, TAIL), :], bcbuf.at[pl.ds(0, TAIL), :], tb_s.at[0], tail_r.at[1], partner
    )
    tail_x_in.wait_recv()
    tail_bc_in.wait_recv()
    local[2].wait()
    local[3].wait()

    @pl.loop(1, PLANE)
    def _(r):
        dta_in(r).wait_recv()
        xa_in(r).wait_recv()

    sub = lax.broadcasted_iota(jnp.int32, (8, 1), 0)
    lane_head = lax.broadcasted_iota(jnp.int32, (1, WIDE), 1) // HEAD_P
    spread = (lax.broadcasted_iota(jnp.int32, (8, WIDE), 0) == lax.broadcasted_iota(jnp.int32, (8, WIDE), 1) // HEAD_P)
    spread = spread.astype(F32)
    a_log = jnp.zeros((8, 1), F32)
    skip = jnp.zeros((1, WIDE), F32)
    for h in range(OWN_HEADS):
        a_log = jnp.where(sub == h, alog_ref[j * OWN_HEADS + h], a_log)
        skip = jnp.where(lane_head == h, dskip_ref[j * OWN_HEADS + h], skip)
    rate = -jnp.exp(a_log)
    rows_i = lax.broadcasted_iota(jnp.int32, (ROWS, ROWS), 0)
    cols_i = lax.broadcasted_iota(jnp.int32, (ROWS, ROWS), 1)
    causal = cols_i <= rows_i
    sums = (rows_i <= cols_i).astype(F32)
    taps_x = taps_x_ref[:, cols(j)].astype(F32)
    taps_bc = taps_bc_ref[...].astype(F32)

    def conv(buf, taps, c):
        raw = buf[pl.ds(pl.multiple_of(c * ROWS, ROWS), ROWS + TAIL), :].astype(F32)
        row = lax.broadcasted_iota(jnp.int32, (ROWS + TAIL, 1), 0) + c * ROWS
        raw = jnp.where(jnp.logical_and(z == 0, row < TAIL), 0.0, raw)
        total = jnp.zeros((ROWS, WIDE), F32)
        for k in range(CONV):
            start = TAIL - CONV + 1 + k
            total = total + taps[k : k + 1, :] * raw[start : start + ROWS, :]
        return silu(total)

    def chunk(c):
        return pl.ds(pl.multiple_of(c * ROWS, ROWS), ROWS)

    def fore(c, carry):
        state, lead = carry
        xs = conv(xbuf, taps_x, c)
        xs_ref[chunk(c), :] = xs
        bc = conv(bcbuf, taps_bc, c)
        b_ref[chunk(c), :] = bc[:, :STATE]
        c_ref[chunk(c), :] = bc[:, STATE:]
        step = softplus(dtbuf[c])
        cum = exact(step * rate, sums)
        step_ref[c] = step
        cum_ref[c] = cum
        states[c] = state
        lead_ref[c] = jnp.broadcast_to(lead, (8, WIDE))
        end = cum[:, ROWS - 1 :]
        weight = exact(jnp.transpose(step * jnp.exp(end - cum)), spread)
        fade = exact(jnp.transpose(jnp.exp(jnp.broadcast_to(end, (8, ROWS)))), spread)[:1, :]
        state = state * fade + dot3(jnp.transpose(bc[:, :STATE]), xs * weight)
        return state, lead * fade

    state, lead = lax.fori_loop(
        0, PLANE, fore, (jnp.zeros((STATE, WIDE), F32), jnp.ones((1, WIDE), F32))
    )
    for k in range(PLANES):
        tsrc[k, pl.ds(0, SPLIT), :] = state[k * SPLIT : (k + 1) * SPLIT, :]
        tsrc[k, pl.ds(SPLIT, 8), :] = jnp.broadcast_to(lead, (8, WIDE))

    def ta(r):
        return remote(tsrc.at[(z + r) % PLANES], trecv.at[z], t_s.at[r], t_r.at[r], in_column(r))

    def ta_in(r):
        slot = trecv.at[from_column(r)]
        return remote(slot, slot, t_s.at[r], t_r.at[r], in_column(r))

    @pl.loop(1, PLANES)
    def _(r):
        ta(r).start()

    ring_step(1)

    def inside(c, _):
        xs = xs_ref[chunk(c), :]
        bmap = b_ref[chunk(c), :]
        cmap = c_ref[chunk(c), :]
        cum = cum_ref[c]
        step = step_ref[c]
        cum_t = jnp.transpose(cum)
        inner = dot3(cmap, bmap, NT)
        mixing = []
        blocks = []
        for h in range(OWN_HEADS):
            gap = cum_t[:, h : h + 1] - cum[h : h + 1, :]
            decay = jnp.where(causal, jnp.exp(jnp.where(causal, gap, 0.0)), 0.0)
            mixing.append(inner * decay * step[h : h + 1, :])
            blocks.append(jnp.where(lane_head == h, xs, 0.0))
        y = dot3(jnp.concatenate(mixing, axis=1), jnp.concatenate(blocks, axis=0))
        grown = exact(jnp.exp(cum_t), spread)
        y = y + grown * dot3(cmap, states[c]) + skip * xs
        y_ref[chunk(c), :] = y
        return 0

    trecv[z] = tsrc[z]
    lax.fori_loop(0, PLANE, inside, 0)

    @pl.loop(1, PLANES)
    def _(r):
        ta_in(r).wait_recv()

    def prefix(k, carry):
        psrc[k] = carry
        return carry * trecv[k, pl.ds(SPLIT, 1), :] + trecv[k, pl.ds(0, SPLIT), :]

    lax.fori_loop(0, PLANES, prefix, jnp.zeros((SPLIT, WIDE), F32))

    def part_rows(k):
        return pl.ds(pl.multiple_of(k * SPLIT, SPLIT), SPLIT)

    def pa(r):
        return remote(psrc.at[(z + r) % PLANES], precv.at[part_rows(z), :], p_s.at[r], p_r.at[r], in_column(r))

    def pa_in(r):
        slot = precv.at[part_rows(from_column(r)), :]
        return remote(slot, slot, p_s.at[r], p_r.at[r], in_column(r))

    @pl.loop(1, PLANES)
    def _(r):
        pa(r).start()

    precv[part_rows(z), :] = psrc[z]
    attend_step(1)
    ring_step(2)
    attend_step(7)

    @pl.loop(1, PLANES)
    def _(r):
        pa_in(r).wait_recv()

    local[4].wait()

    @pl.loop(1, PLANE)
    def _(r):
        ga_in(r).wait_recv()

    def finish(c, _):
        grown = exact(jnp.transpose(jnp.exp(cum_ref[c])), spread) * lead_ref[c][:1, :]
        y = y_ref[chunk(c), :] + grown * dot3(c_ref[chunk(c), :], precv[...])
        gated = y * silu(gbuf[chunk(c), :].astype(F32))
        y_ref[chunk(c), :] = gated
        ss_ref[pl.ds(c, 1), :] = exact(jnp.ones((8, WIDE), F32), gated * gated, NT)[:1, :]
        return 0

    lax.fori_loop(0, PLANE, finish, 0)

    def ma(r):
        return pltpu.make_async_remote_copy(
            src_ref=ss_ref,
            dst_ref=ssm_ref.at[r],
            send_sem=m_s.at[r],
            recv_sem=m_r.at[r],
            device_id={"mp": (mine_mp + r) % 4},
            device_id_type=MESH,
        )

    @pl.loop(1, 4)
    def _(r):
        ma(r).start()

    attend_step(2)
    ring_step(3)

    @pl.loop(1, 4)
    def _(r):
        ma(r).wait_recv()

    ss2_ref[...] = (ss_ref[...] + ssm_ref[1]) + (ssm_ref[2] + ssm_ref[3])

    def na(r):
        return remote(ss2_ref, ssp_ref.at[r], n_s.at[r], n_r.at[r], in_plane(r))

    @pl.loop(1, PLANE)
    def _(r):
        na(r).start()

    attend_step(6)

    @pl.loop(1, PLANE)
    def _(r):
        na(r).wait_recv()

    squares = ss2_ref[...]
    for r in range(1, PLANE):
        squares = squares + ssp_ref[r]
    inverse = jnp.transpose(lax.rsqrt(squares / D_INNER + 1e-05))
    gain = gain_ref[:, cols(j)]
    which = lax.broadcasted_iota(jnp.int32, (ROWS, PLANE), 1)

    def oa(r):
        return remote(osrc.at[r], mix_hbm.at[:, cols(j)], o_s.at[r], o_r.at[r], in_plane(r))

    def oa_in(r):
        return remote(osrc.at[r], mix_hbm.at[:, cols(from_plane(r))], o_s.at[r], o_r.at[r], in_plane(r))

    own_out = pltpu.make_async_copy(osrc.at[0], mix_hbm.at[:, cols(j)], local_sem.at[5])

    def norm(r, _):
        c = (j + r) % PLANE
        by = jnp.sum(jnp.where(which == c, inverse, 0.0), axis=1, keepdims=True)
        osrc[r] = (y_ref[chunk(c), :] * by * gain).astype(BF16)

        @pl.when(r > 0)
        def _():
            oa(r).start()

        return 0

    lax.fori_loop(0, PLANE, norm, 0)
    own_out.start()

    attend_step(3)
    ring_step(4)
    attend_step(5)
    attend_step(4)

    for h in range(Q_HEADS):
        acc = acc_ref[pl.ds(h * ROWS, ROWS), :]
        obuf[:, h * 128 : (h + 1) * 128] = (acc[:, :HEAD_WIDTH] / acc[:, HEAD_WIDTH:]).astype(BF16)
    att_out = pltpu.make_async_copy(obuf, att_hbm, local_sem.at[6])
    att_out.start()

    @pl.loop(1, CHIPS)
    def _(r):
        kvx(r).wait_send()
        bcx(r).wait_send()
        bcp(r).wait_send()
        ma(r).wait_send()

    bcp_own.wait_send()

    @pl.loop(1, PLANE)
    def _(r):
        dta(r).wait_send()
        xa(r).wait_send()
        ga(r).wait_send()
        ta(r).wait_send()
        pa(r).wait_send()
        na(r).wait_send()
        oa(r).wait_send()

    @pl.when(j == PLANE - 1)
    def _():
        @pl.loop(0, PLANE)
        def _(d):
            tail_x(d).wait_send()
            tail_bc(d).wait_send()

    for s in range(1, 5):
        up(s).wait_send()
    for s in range(1, 4):
        down(s).wait_send()
    for i in range(PLANES):
        share((z + PLANES - i) % PLANES, i).wait_send()

    @pl.loop(1, PLANE)
    def _(r):
        oa_in(r).wait_recv()

    own_out.wait()
    att_out.wait()


def body(
    x_in, gate_z, bc_in, dt_raw, a_log, d_skip, conv_x, conv_bc, norm_gain, queries, key_value_pairs
):
    anywhere = pl.BlockSpec(memory_space=pl.ANY)
    vmem = pl.BlockSpec(memory_space=pltpu.VMEM)
    smem = pl.BlockSpec(memory_space=pltpu.SMEM)
    dma = pltpu.SemaphoreType.DMA
    scratch = [
        pltpu.VMEM((PLANES, 2, TOK, HEAD_WIDTH), BF16),
        pltpu.VMEM((TAIL + TOK, WIDE), BF16),
        pltpu.VMEM((TOK, WIDE), BF16),
        pltpu.VMEM((TAIL + TOK, WIDE), BF16),
        pltpu.VMEM((PLANE, 8, ROWS), F32),
        pltpu.VMEM((PLANE, 8, ROWS), F32),
        pltpu.VMEM((TOK, WIDE), F32),
        pltpu.VMEM((TOK, STATE), F32),
        pltpu.VMEM((TOK, STATE), F32),
        pltpu.VMEM((PLANE, 8, ROWS), F32),
        pltpu.VMEM((PLANE, 8, ROWS), F32),
        pltpu.VMEM((PLANE, 8, WIDE), F32),
        pltpu.VMEM((PLANE, STATE, WIDE), F32),
        pltpu.VMEM((TOK, WIDE), F32),
        pltpu.VMEM((PLANES, SPLIT + 8, WIDE), F32),
        pltpu.VMEM((PLANES, SPLIT + 8, WIDE), F32),
        pltpu.VMEM((PLANES, SPLIT, WIDE), F32),
        pltpu.VMEM((STATE, WIDE), F32),
        pltpu.VMEM((PLANE, ROWS), F32),
        pltpu.VMEM((4, PLANE, ROWS), F32),
        pltpu.VMEM((PLANE, ROWS), F32),
        pltpu.VMEM((PLANE, PLANE, ROWS), F32),
        pltpu.VMEM((PLANE, ROWS, WIDE), BF16),
        pltpu.VMEM((Q_HEADS * ROWS, HEAD_WIDTH), BF16),
        pltpu.VMEM((Q_HEADS * ROWS, HEAD_WIDTH), F32),
        pltpu.VMEM((Q_HEADS * ROWS, 2 * HEAD_WIDTH), F32),
        pltpu.VMEM((ROWS, Q_HEADS * HEAD_WIDTH), BF16),
        dma((7,)),
        dma((Q_HEADS,)),
        dma((8,)),
        dma((8,)),
        dma((8,)),
        dma((8,)),
        dma((8,)),
        dma((8,)),
        dma((4,)),
        dma((4,)),
        dma((4,)),
        dma((4,)),
        dma((4,)),
        dma((4,)),
        dma((8,)),
        dma((8,)),
        dma((5,)),
        dma((5,)),
        dma((4,)),
        dma((4,)),
        dma((8,)),
        dma((8,)),
        dma((2,)),
        dma((8,)),
        dma((8,)),
        dma((8,)),
        dma((8,)),
        dma((4,)),
        dma((4,)),
        dma((8,)),
        dma((8,)),
        dma((8,)),
        dma((8,)),
    ]
    return pl.pallas_call(
        kernel,
        out_shape=(
            jax.ShapeDtypeStruct(x_in.shape, BF16),
            jax.ShapeDtypeStruct(queries.shape, BF16),
        ),
        in_specs=[
            anywhere,
            anywhere,
            anywhere,
            vmem,
            smem,
            smem,
            vmem,
            vmem,
            vmem,
            anywhere,
            anywhere,
        ],
        out_specs=(anywhere, anywhere),
        scratch_shapes=scratch,
        compiler_params=pltpu.CompilerParams(
            collective_id=0, has_side_effects=True, vmem_limit_bytes=60 * 1024 * 1024
        ),
    )(
        x_in,
        gate_z,
        bc_in,
        dt_raw,
        a_log,
        d_skip,
        conv_x,
        conv_bc,
        norm_gain[None, :],
        queries,
        key_value_pairs,
    )


def solution(mesh):
    placed = (
        P("seq", "mp"),
        P("seq", "mp"),
        P("seq", None),
        P("seq", "mp"),
        P("mp"),
        P("mp"),
        P(None, "mp"),
        P(),
        P("mp"),
        P("seq", "mp"),
        P(None, "seq", "mp"),
    )
    return jax.shard_map(
        body,
        mesh=mesh,
        in_specs=placed,
        out_specs=(P("seq", "mp"), P("seq", "mp")),
        check_vma=False,
    )
```

```python
import jax
import jax.numpy as jnp
from jax import lax
from jax.experimental import pallas as pl
from jax.experimental.pallas import tpu as pltpu
from jax.sharding import PartitionSpec as P

HEAD_P = 64
STATE = 128
CONV = 4
HEAD_WIDTH = 128
D_INNER = 8192

ROWS = 128
PLANE = 8
PLANES = 8
CHIPS = 4
TOK = PLANE * ROWS
WIDE = 256
OWN_HEADS = 4
TAIL = 16
Q_HEADS = 8
SPLIT = 16

MESH = pl.DeviceIdType.MESH
F32 = jnp.float32
BF16 = jnp.bfloat16
NN = (((1,), (0,)), ((), ()))
NT = (((1,), (1,)), ((), ()))


def dot1(a, b, dims=NN):
    return lax.dot_general(a, b, dims, preferred_element_type=F32)


def halves(v):
    high = v.astype(BF16)
    return high, (v - high.astype(F32)).astype(BF16)


def left3(a):
    high, low = halves(a)
    return jnp.concatenate([high, low, high], axis=1)


def right3(b, axis):
    high, low = halves(b)
    return jnp.concatenate([high, high, low], axis=axis)


def dot3(a, b, dims=NN):
    return dot1(left3(a), right3(b, 0 if dims == NN else 1), dims)


def widen(rows, spread):
    high = rows.astype(BF16).astype(F32)
    both = jnp.concatenate([high, rows - high], axis=0)
    return dot1(jnp.transpose(both).astype(BF16), spread)


def running_sums(rows, sums):
    high = rows.astype(BF16).astype(F32)
    rest = rows - high
    middle = rest.astype(BF16).astype(F32)
    parts = jnp.concatenate([high, middle, rest - middle], axis=0).astype(BF16)
    total = dot1(parts, sums)
    return total[:8] + (total[8:16] + total[16:])


def silu(v):
    return v / (1.0 + jnp.exp(-v))


def softplus(v):
    u = jnp.exp(-jnp.abs(v))
    w = 1.0 + u
    small = w == 1.0
    tail = jnp.where(small, u, jnp.log(w) * (u / jnp.where(small, 1.0, w - 1.0)))
    return jnp.maximum(v, 0.0) + tail


def kernel(
    x_hbm,
    gate_hbm,
    bc_hbm,
    dt_ref,
    alog_ref,
    dskip_ref,
    taps_x_ref,
    taps_bc_ref,
    gain_ref,
    q_hbm,
    kv_hbm,
    mix_hbm,
    att_hbm,
    kvbuf,
    xbuf,
    gbuf,
    bcbuf,
    dtsrc,
    dtbuf,
    xs_ref,
    b_ref,
    c_ref,
    cum_ref,
    step_ref,
    lead_ref,
    grown_ref,
    states,
    y_ref,
    tsrc,
    trecv,
    psrc,
    precv,
    ss_ref,
    ssp_ref,
    osrc,
    qbuf,
    peak_ref,
    acc_ref,
    obuf,
    local_sem,
    q_sem,
    x_s,
    x_r,
    dt_s,
    dt_r,
    g_s,
    g_r,
    bcx_s,
    bcx_r,
    bcp_s,
    bcp_r,
    kvx_s,
    kvx_r,
    kvp_s,
    kvp_r,
    up_s,
    up_r,
    dn_s,
    dn_r,
    tx_s,
    tb_s,
    tail_r,
    t_s,
    t_r,
    p_s,
    p_r,
    n_s,
    n_r,
    o_s,
    o_r,
):
    me = lax.axis_index("seq")
    mine_mp = lax.axis_index("mp")
    z = me // PLANE
    j = me % PLANE
    xc = j // 2
    core = j % 2
    base = z * PLANE
    partner = base + xc * 2 + (1 - core)
    above = ((z + 1) % PLANES) * PLANE
    below = ((z + PLANES - 1) % PLANES) * PLANE

    def remote(src, dst, ss, rs, seq):
        return pltpu.make_async_remote_copy(
            src_ref=src, dst_ref=dst, send_sem=ss, recv_sem=rs, device_id={"seq": seq}, device_id_type=MESH
        )

    def in_plane(r):
        return base + (j + r) % PLANE

    def on_chip(r):
        return base + ((xc + r) % CHIPS) * 2 + core

    def in_column(r):
        return ((z + r) % PLANES) * PLANE + j

    def from_plane(r):
        return (j + PLANE - r) % PLANE

    def from_column(r):
        return (z + PLANES - r) % PLANES

    barrier = pltpu.get_barrier_semaphore()

    def greet(seq):
        pl.semaphore_signal(barrier, inc=1, device_id={"seq": seq}, device_id_type=MESH)

    @pl.loop(1, 4 * PLANE)
    def _(q):
        pl.semaphore_signal(
            barrier,
            inc=1,
            device_id={"seq": in_plane(q % PLANE), "mp": (mine_mp + q // PLANE) % 4},
            device_id_type=MESH,
        )

    @pl.loop(1, PLANE)
    def _(r):
        greet(in_column(r))

    @pl.when(j == PLANE - 1)
    def _():
        @pl.loop(0, PLANE - 1)
        def _(d):
            greet(above + d)

    @pl.when(j != PLANE - 1)
    def _():
        greet(below + PLANE - 1)

    dt_t = dt_ref[...]
    for d in range(PLANE):
        dtsrc[d, pl.ds(0, OWN_HEADS), :] = dt_t[d * OWN_HEADS : (d + 1) * OWN_HEADS]
        dtsrc[d, pl.ds(OWN_HEADS, OWN_HEADS), :] = jnp.zeros((OWN_HEADS, ROWS), F32)

    my_rows = pl.ds(pl.multiple_of(TAIL + j * ROWS, TAIL), ROWS)
    kv_off = pl.multiple_of(core * 512 + xc * ROWS, ROWS)
    kv_mine = kvbuf.at[z, :, pl.ds(kv_off, ROWS), :]

    def cols(d):
        return pl.ds(pl.multiple_of(d * WIDE, WIDE), WIDE)

    local = [
        pltpu.make_async_copy(kv_hbm, kv_mine, local_sem.at[0]),
        pltpu.make_async_copy(bc_hbm, bcbuf.at[my_rows, :], local_sem.at[1]),
        pltpu.make_async_copy(x_hbm.at[:, cols(j)], xbuf.at[my_rows, :], local_sem.at[2]),
        pltpu.make_async_copy(dtsrc.at[j], dtbuf.at[j], local_sem.at[3]),
        pltpu.make_async_copy(
            gate_hbm.at[:, cols(j)], gbuf.at[pl.ds(pl.multiple_of(j * ROWS, ROWS), ROWS), :], local_sem.at[4]
        ),
    ]
    for copy in local:
        copy.start()
    for h in range(Q_HEADS):
        pltpu.make_async_copy(q_hbm.at[:, pl.ds(h * 128, 128)], qbuf.at[pl.ds(h * ROWS, ROWS), :], q_sem.at[h]).start()

    pl.semaphore_wait(barrier, 5 * PLANE - 2 + jnp.where(j == PLANE - 1, PLANE - 1, 1))

    def kvx(r):
        return remote(kv_hbm, kv_mine, kvx_s.at[r], kvx_r.at[r], on_chip(r))

    def kvx_in(r):
        off = pl.multiple_of(core * 512 + ((xc + CHIPS - r) % CHIPS) * ROWS, ROWS)
        slot = kvbuf.at[z, :, pl.ds(off, ROWS), :]
        return remote(slot, slot, kvx_s.at[r], kvx_r.at[r], partner)

    def bcx(r):
        return remote(bc_hbm, bcbuf.at[my_rows, :], bcx_s.at[r], bcx_r.at[r], on_chip(r))

    def bc_slot(r, half):
        owner = ((xc + CHIPS - r) % CHIPS) * 2 + half
        return bcbuf.at[pl.ds(pl.multiple_of(TAIL + owner * ROWS, TAIL), ROWS), :]

    def bcx_in(r):
        slot = bc_slot(r, core)
        return remote(slot, slot, bcx_s.at[r], bcx_r.at[r], partner)

    def bcp(r):
        slot = bc_slot(r, core)
        return remote(slot, slot, bcp_s.at[r], bcp_r.at[r], partner)

    def bcp_in(r):
        slot = bc_slot(r, 1 - core)
        return remote(slot, slot, bcp_s.at[r], bcp_r.at[r], partner)

    bcp_own = remote(bc_hbm, bcbuf.at[my_rows, :], bcp_s.at[0], bcp_r.at[0], partner)

    def xa(r):
        return remote(
            x_hbm.at[:, cols((j + r) % PLANE)], xbuf.at[my_rows, :], x_s.at[r], x_r.at[r], in_plane(r)
        )

    def xa_in(r):
        slot = xbuf.at[pl.ds(pl.multiple_of(TAIL + from_plane(r) * ROWS, TAIL), ROWS), :]
        return remote(slot, slot, x_s.at[r], x_r.at[r], in_plane(r))

    def dta(r):
        return remote(dtsrc.at[(j + r) % PLANE], dtbuf.at[j], dt_s.at[r], dt_r.at[r], in_plane(r))

    def dta_in(r):
        slot = dtbuf.at[from_plane(r)]
        return remote(slot, slot, dt_s.at[r], dt_r.at[r], in_plane(r))

    def ga(r):
        slot = gbuf.at[pl.ds(pl.multiple_of(j * ROWS, ROWS), ROWS), :]
        return remote(gate_hbm.at[:, cols((j + r) % PLANE)], slot, g_s.at[r], g_r.at[r], in_plane(r))

    def ga_in(r):
        slot = gbuf.at[pl.ds(pl.multiple_of(from_plane(r) * ROWS, ROWS), ROWS), :]
        return remote(slot, slot, g_s.at[r], g_r.at[r], in_plane(r))

    last_rows = pl.ds(ROWS - TAIL, TAIL)

    def tail_x(d):
        return remote(
            x_hbm.at[last_rows, cols(d)], xbuf.at[pl.ds(0, TAIL), :], tx_s.at[d], tail_r.at[0], above + d
        )

    def tail_bc(d):
        return remote(
            bc_hbm.at[last_rows, :], bcbuf.at[pl.ds(0, TAIL), :], tb_s.at[d], tail_r.at[1], above + d
        )

    @pl.loop(1, CHIPS)
    def _(r):
        kvx(r).start()

    @pl.loop(1, CHIPS)
    def _(r):
        bcx(r).start()

    bcp_own.start()

    @pl.when(j == PLANE - 1)
    def _():
        @pl.loop(0, PLANE)
        def _(d):
            tail_x(d).start()
            tail_bc(d).start()

    @pl.loop(1, PLANE)
    def _(r):
        dta(r).start()
        xa(r).start()

    @pl.loop(1, PLANE)
    def _(r):
        ga(r).start()

    def column(zz, half):
        return kvbuf.at[zz, :, pl.ds(pl.multiple_of(half * 512, 512), 512), :]

    def up(s):
        part = column((z + PLANES - s + 1) % PLANES, core)
        return remote(part, part, up_s.at[s], up_r.at[s], above + j)

    def up_in(s):
        part = column((z + PLANES - s) % PLANES, core)
        return remote(part, part, up_s.at[s], up_r.at[s], above + j)

    def down(s):
        part = column((z + s - 1) % PLANES, core)
        return remote(part, part, dn_s.at[s], dn_r.at[s], below + j)

    def down_in(s):
        part = column((z + s) % PLANES, core)
        return remote(part, part, dn_s.at[s], dn_r.at[s], below + j)

    def share(zz, i):
        part = column(zz, core)
        return remote(part, part, kvp_s.at[i], kvp_r.at[i], partner)

    def share_in(zz, i):
        part = column(zz, 1 - core)
        return remote(part, part, kvp_s.at[i], kvp_r.at[i], partner)

    local[0].wait()

    @pl.loop(1, CHIPS)
    def _(r):
        kvx_in(r).wait_recv()

    up(1).start()
    down(1).start()
    share(z, 0).start()

    def ring_step(s):
        up_in(s).wait_recv()
        if s < 4:
            up(s + 1).start()
        share((z + PLANES - s) % PLANES, s).start()
        if s < 4:
            down_in(s).wait_recv()
            if s < 3:
                down(s + 1).start()
            share((z + s) % PLANES, 8 - s).start()

    factor = (HEAD_WIDTH ** (-0.5)) * 1.4426950408889634
    tile = 512

    def attend(zz, own):
        @pl.loop(0, Q_HEADS * ROWS // tile)
        def _(t):
            rows = pl.ds(pl.multiple_of(t * tile, tile), tile)
            q = qbuf[rows, :]
            score = dot1(q, kvbuf[zz, 0], NT)
            if own:
                lane = lax.broadcasted_iota(jnp.int32, (1, TOK), 1)
                spot = (((lane % 512) // ROWS) * 2 + lane // 512) * ROWS + lane % ROWS
                place = j * ROWS + lax.broadcasted_iota(jnp.int32, (tile, 1), 0) % ROWS
                score = jnp.where(spot <= place, score, -1e30)
                peak = jnp.max(score, axis=1, keepdims=True)
            else:
                before = peak_ref[rows, :][:, :1]
                peak = jnp.maximum(before, jnp.max(score, axis=1, keepdims=True))
            weights = jnp.exp2((score - peak) * factor)
            high, low = halves(weights)
            value = jnp.concatenate([kvbuf[zz, 1], jnp.ones((TOK, HEAD_WIDTH), BF16)], axis=1)
            part = dot1(high, value) + dot1(low, value)
            if own:
                acc_ref[rows, :] = part
            else:
                acc_ref[rows, :] = acc_ref[rows, :] * jnp.exp2((before - peak) * factor) + part
            peak_ref[rows, :] = jnp.broadcast_to(peak, (tile, HEAD_WIDTH))

    def attend_step(i):
        zz = (z + PLANES - i) % PLANES
        share_in(zz, i).wait_recv()

        @pl.when(i <= z)
        def _():
            attend(zz, False)

    for h in range(Q_HEADS):
        pltpu.make_async_copy(q_hbm.at[:, pl.ds(h * 128, 128)], qbuf.at[pl.ds(h * ROWS, ROWS), :], q_sem.at[h]).wait()
    share_in(z, 0).wait_recv()

    local[1].wait()

    @pl.loop(1, CHIPS)
    def _(r):
        bcx_in(r).wait_recv()
        bcp(r).start()

    attend(z, True)

    @pl.loop(0, CHIPS)
    def _(r):
        bcp_in(r).wait_recv()

    tail_x_in = remote(
        xbuf.at[pl.ds(0, TAIL), :], xbuf.at[pl.ds(0, TAIL), :], tx_s.at[0], tail_r.at[0], partner
    )
    tail_bc_in = remote(
        bcbuf.at[pl.ds(0, TAIL), :], bcbuf.at[pl.ds(0, TAIL), :], tb_s.at[0], tail_r.at[1], partner
    )
    tail_x_in.wait_recv()
    tail_bc_in.wait_recv()
    local[2].wait()
    local[3].wait()

    @pl.loop(1, PLANE)
    def _(r):
        dta_in(r).wait_recv()
        xa_in(r).wait_recv()

    sub = lax.broadcasted_iota(jnp.int32, (8, 1), 0)
    lane_head = lax.broadcasted_iota(jnp.int32, (1, WIDE), 1) // HEAD_P
    spread = lax.broadcasted_iota(jnp.int32, (16, WIDE), 0) % 8 == lax.broadcasted_iota(jnp.int32, (16, WIDE), 1) // HEAD_P
    spread = spread.astype(F32).astype(BF16)
    a_log = jnp.zeros((8, 1), F32)
    skip = jnp.zeros((1, WIDE), F32)
    for h in range(OWN_HEADS):
        a_log = jnp.where(sub == h, alog_ref[j * OWN_HEADS + h], a_log)
        skip = jnp.where(lane_head == h, dskip_ref[j * OWN_HEADS + h], skip)
    rate = -jnp.exp(a_log)
    rows_i = lax.broadcasted_iota(jnp.int32, (ROWS, ROWS), 0)
    cols_i = lax.broadcasted_iota(jnp.int32, (ROWS, ROWS), 1)
    causal = cols_i <= rows_i
    sums = (rows_i <= cols_i).astype(F32).astype(BF16)
    taps_x = taps_x_ref[:, cols(j)].astype(F32)
    taps_bc = taps_bc_ref[...].astype(F32)

    def conv(buf, taps, c):
        raw = buf[pl.ds(pl.multiple_of(c * ROWS, ROWS), ROWS + TAIL), :].astype(F32)
        row = lax.broadcasted_iota(jnp.int32, (ROWS + TAIL, 1), 0) + c * ROWS
        raw = jnp.where(jnp.logical_and(z == 0, row < TAIL), 0.0, raw)
        total = jnp.zeros((ROWS, WIDE), F32)
        for k in range(CONV):
            start = TAIL - CONV + 1 + k
            total = total + taps[k : k + 1, :] * raw[start : start + ROWS, :]
        return silu(total)

    def chunk(c):
        return pl.ds(pl.multiple_of(c * ROWS, ROWS), ROWS)

    def fore(c, carry):
        state, lead = carry
        xs = conv(xbuf, taps_x, c)
        xs_ref[chunk(c), :] = xs
        bc = conv(bcbuf, taps_bc, c)
        b_ref[chunk(c), :] = bc[:, :STATE]
        c_ref[chunk(c), :] = bc[:, STATE:]
        step = softplus(dtbuf[c])
        cum = running_sums(step * rate, sums)
        step_ref[c] = step
        cum_ref[c] = cum
        states[c] = state
        lead_ref[c] = jnp.broadcast_to(lead, (8, WIDE))
        end = cum[:, ROWS - 1 :]
        weight = widen(step * jnp.exp(end - cum), spread)
        grown = widen(jnp.exp(cum), spread)
        grown_ref[chunk(c), :] = grown
        fade = grown[ROWS - 1 :, :]
        state = state * fade + dot3(jnp.transpose(bc[:, :STATE]), xs * weight)
        return state, lead * fade

    state, lead = lax.fori_loop(
        0, PLANE, fore, (jnp.zeros((STATE, WIDE), F32), jnp.ones((1, WIDE), F32))
    )
    for k in range(PLANES):
        tsrc[k, pl.ds(0, SPLIT), :] = state[k * SPLIT : (k + 1) * SPLIT, :]
        tsrc[k, pl.ds(SPLIT, 8), :] = jnp.broadcast_to(lead, (8, WIDE))

    def ta(r):
        return remote(tsrc.at[(z + r) % PLANES], trecv.at[z], t_s.at[r], t_r.at[r], in_column(r))

    def ta_in(r):
        slot = trecv.at[from_column(r)]
        return remote(slot, slot, t_s.at[r], t_r.at[r], in_column(r))

    @pl.loop(1, PLANES)
    def _(r):
        ta(r).start()

    ring_step(1)

    def inside(c, _):
        xs = xs_ref[chunk(c), :]
        bmap = b_ref[chunk(c), :]
        cmap = c_ref[chunk(c), :]
        cum = cum_ref[c]
        step = step_ref[c]
        cum_t = jnp.transpose(cum)
        inner = dot3(cmap, bmap, NT)
        mixing = []
        blocks = []
        for h in range(OWN_HEADS):
            gap = cum_t[:, h : h + 1] - cum[h : h + 1, :]
            decay = jnp.where(causal, jnp.exp(jnp.where(causal, gap, 0.0)), 0.0)
            mixing.append(inner * decay * step[h : h + 1, :])
            blocks.append(jnp.where(lane_head == h, xs, 0.0))
        y = dot3(jnp.concatenate(mixing, axis=1), jnp.concatenate(blocks, axis=0))
        y = y + grown_ref[chunk(c), :] * dot3(cmap, states[c]) + skip * xs
        y_ref[chunk(c), :] = y
        return 0

    trecv[z] = tsrc[z]
    lax.fori_loop(0, PLANE, inside, 0)

    @pl.loop(1, PLANES)
    def _(r):
        ta_in(r).wait_recv()

    def prefix(k, carry):
        psrc[k] = carry
        return carry * trecv[k, pl.ds(SPLIT, 1), :] + trecv[k, pl.ds(0, SPLIT), :]

    lax.fori_loop(0, PLANES, prefix, jnp.zeros((SPLIT, WIDE), F32))

    def part_rows(k):
        return pl.ds(pl.multiple_of(k * SPLIT, SPLIT), SPLIT)

    def pa(r):
        return remote(psrc.at[(z + r) % PLANES], precv.at[part_rows(z), :], p_s.at[r], p_r.at[r], in_column(r))

    def pa_in(r):
        slot = precv.at[part_rows(from_column(r)), :]
        return remote(slot, slot, p_s.at[r], p_r.at[r], in_column(r))

    @pl.loop(1, PLANES)
    def _(r):
        pa(r).start()

    precv[part_rows(z), :] = psrc[z]
    attend_step(1)
    ring_step(2)
    attend_step(7)

    @pl.loop(1, PLANES)
    def _(r):
        pa_in(r).wait_recv()

    local[4].wait()

    @pl.loop(1, PLANE)
    def _(r):
        ga_in(r).wait_recv()

    which = lax.broadcasted_iota(jnp.int32, (ROWS, PLANE), 1)
    before = right3(precv[...], 0)

    def finish(c, squares):
        grown = grown_ref[chunk(c), :] * lead_ref[c][:1, :]
        y = y_ref[chunk(c), :] + grown * dot1(left3(c_ref[chunk(c), :]), before)
        gated = y * silu(gbuf[chunk(c), :].astype(F32))
        y_ref[chunk(c), :] = gated
        return jnp.where(which == c, jnp.sum(gated * gated, axis=1, keepdims=True), squares)

    ss_ref[...] = jnp.transpose(lax.fori_loop(0, PLANE, finish, jnp.zeros((ROWS, PLANE), F32)))

    def na(q):
        return pltpu.make_async_remote_copy(
            src_ref=ss_ref,
            dst_ref=ssp_ref.at[q],
            send_sem=n_s.at[q],
            recv_sem=n_r.at[q],
            device_id={"seq": in_plane(q % PLANE), "mp": (mine_mp + q // PLANE) % 4},
            device_id_type=MESH,
        )

    @pl.loop(1, 4 * PLANE)
    def _(q):
        na(q).start()

    attend_step(2)
    ring_step(3)
    attend_step(6)

    @pl.loop(1, 4 * PLANE)
    def _(q):
        na(q).wait_recv()

    squares = ss_ref[...]
    for q in range(1, 4 * PLANE):
        squares = squares + ssp_ref[q]
    inverse = jnp.transpose(lax.rsqrt(squares / D_INNER + 1e-05))
    gain = gain_ref[:, cols(j)]

    def oa(r):
        return remote(osrc.at[r], mix_hbm.at[:, cols(j)], o_s.at[r], o_r.at[r], in_plane(r))

    def oa_in(r):
        return remote(osrc.at[r], mix_hbm.at[:, cols(from_plane(r))], o_s.at[r], o_r.at[r], in_plane(r))

    own_out = pltpu.make_async_copy(osrc.at[0], mix_hbm.at[:, cols(j)], local_sem.at[5])

    def norm(r, _):
        c = (j + r) % PLANE
        by = jnp.sum(jnp.where(which == c, inverse, 0.0), axis=1, keepdims=True)
        osrc[r] = (y_ref[chunk(c), :] * by * gain).astype(BF16)

        @pl.when(r > 0)
        def _():
            oa(r).start()

        return 0

    lax.fori_loop(0, PLANE, norm, 0)
    own_out.start()

    attend_step(3)
    ring_step(4)
    attend_step(5)
    attend_step(4)

    for h in range(Q_HEADS):
        acc = acc_ref[pl.ds(h * ROWS, ROWS), :]
        obuf[:, h * 128 : (h + 1) * 128] = (acc[:, :HEAD_WIDTH] / acc[:, HEAD_WIDTH:]).astype(BF16)
    att_out = pltpu.make_async_copy(obuf, att_hbm, local_sem.at[6])
    att_out.start()

    @pl.loop(1, CHIPS)
    def _(r):
        kvx(r).wait_send()
        bcx(r).wait_send()
        bcp(r).wait_send()

    bcp_own.wait_send()

    @pl.loop(1, 4 * PLANE)
    def _(q):
        na(q).wait_send()

    @pl.loop(1, PLANE)
    def _(r):
        dta(r).wait_send()
        xa(r).wait_send()
        ga(r).wait_send()
        ta(r).wait_send()
        pa(r).wait_send()
        oa(r).wait_send()

    @pl.when(j == PLANE - 1)
    def _():
        @pl.loop(0, PLANE)
        def _(d):
            tail_x(d).wait_send()
            tail_bc(d).wait_send()

    for s in range(1, 5):
        up(s).wait_send()
    for s in range(1, 4):
        down(s).wait_send()
    for i in range(PLANES):
        share((z + PLANES - i) % PLANES, i).wait_send()

    @pl.loop(1, PLANE)
    def _(r):
        oa_in(r).wait_recv()

    own_out.wait()
    att_out.wait()


def body(
    x_in, gate_z, bc_in, dt_raw, a_log, d_skip, conv_x, conv_bc, norm_gain, queries, key_value_pairs
):
    anywhere = pl.BlockSpec(memory_space=pl.ANY)
    vmem = pl.BlockSpec(memory_space=pltpu.VMEM)
    smem = pl.BlockSpec(memory_space=pltpu.SMEM)
    dma = pltpu.SemaphoreType.DMA
    scratch = [
        pltpu.VMEM((PLANES, 2, TOK, HEAD_WIDTH), BF16),
        pltpu.VMEM((TAIL + TOK, WIDE), BF16),
        pltpu.VMEM((TOK, WIDE), BF16),
        pltpu.VMEM((TAIL + TOK, WIDE), BF16),
        pltpu.VMEM((PLANE, 8, ROWS), F32),
        pltpu.VMEM((PLANE, 8, ROWS), F32),
        pltpu.VMEM((TOK, WIDE), F32),
        pltpu.VMEM((TOK, STATE), F32),
        pltpu.VMEM((TOK, STATE), F32),
        pltpu.VMEM((PLANE, 8, ROWS), F32),
        pltpu.VMEM((PLANE, 8, ROWS), F32),
        pltpu.VMEM((PLANE, 8, WIDE), F32),
        pltpu.VMEM((TOK, WIDE), F32),
        pltpu.VMEM((PLANE, STATE, WIDE), F32),
        pltpu.VMEM((TOK, WIDE), F32),
        pltpu.VMEM((PLANES, SPLIT + 8, WIDE), F32),
        pltpu.VMEM((PLANES, SPLIT + 8, WIDE), F32),
        pltpu.VMEM((PLANES, SPLIT, WIDE), F32),
        pltpu.VMEM((STATE, WIDE), F32),
        pltpu.VMEM((PLANE, ROWS), F32),
        pltpu.VMEM((4 * PLANE, PLANE, ROWS), F32),
        pltpu.VMEM((PLANE, ROWS, WIDE), BF16),
        pltpu.VMEM((Q_HEADS * ROWS, HEAD_WIDTH), BF16),
        pltpu.VMEM((Q_HEADS * ROWS, HEAD_WIDTH), F32),
        pltpu.VMEM((Q_HEADS * ROWS, 2 * HEAD_WIDTH), F32),
        pltpu.VMEM((ROWS, Q_HEADS * HEAD_WIDTH), BF16),
        dma((7,)),
        dma((Q_HEADS,)),
        dma((8,)),
        dma((8,)),
        dma((8,)),
        dma((8,)),
        dma((8,)),
        dma((8,)),
        dma((4,)),
        dma((4,)),
        dma((4,)),
        dma((4,)),
        dma((4,)),
        dma((4,)),
        dma((8,)),
        dma((8,)),
        dma((5,)),
        dma((5,)),
        dma((4,)),
        dma((4,)),
        dma((8,)),
        dma((8,)),
        dma((2,)),
        dma((8,)),
        dma((8,)),
        dma((8,)),
        dma((8,)),
        dma((32,)),
        dma((32,)),
        dma((8,)),
        dma((8,)),
    ]
    return pl.pallas_call(
        kernel,
        out_shape=(
            jax.ShapeDtypeStruct(x_in.shape, BF16),
            jax.ShapeDtypeStruct(queries.shape, BF16),
        ),
        in_specs=[
            anywhere,
            anywhere,
            anywhere,
            vmem,
            smem,
            smem,
            vmem,
            vmem,
            vmem,
            anywhere,
            anywhere,
        ],
        out_specs=(anywhere, anywhere),
        scratch_shapes=scratch,
        compiler_params=pltpu.CompilerParams(
            collective_id=0, has_side_effects=True, vmem_limit_bytes=60 * 1024 * 1024
        ),
    )(
        x_in,
        gate_z,
        bc_in,
        dt_raw.T,
        a_log,
        d_skip,
        conv_x,
        conv_bc,
        norm_gain[None, :],
        queries,
        key_value_pairs,
    )


def solution(mesh):
    placed = (
        P("seq", "mp"),
        P("seq", "mp"),
        P("seq", None),
        P("seq", "mp"),
        P("mp"),
        P("mp"),
        P(None, "mp"),
        P(),
        P("mp"),
        P("seq", "mp"),
        P(None, "seq", "mp"),
    )
    return jax.shard_map(
        body,
        mesh=mesh,
        in_specs=placed,
        out_specs=(P("seq", "mp"), P("seq", "mp")),
        check_vma=False,
    )
```
